128 devices in a mesh: ctx: 32 (over x, z, y_lo), fsdp: 4 (over y_hi, core).
Axes of the slice: x: 4, y: 4 (y_hi: 2, y_lo: 2; y = y_hi * 2 + y_lo), z: 4, core: 2. Of those that a mesh axis runs over, the one named last changes fastest.
Arguments:
- x_cur: bfloat16 [4, 8192, 2048], P('fsdp', 'ctx'), may hold values from -6 to 6
- x_next: bfloat16 [4, 8192, 2048], P('fsdp', 'ctx'), may hold values from -6 to 6
- cot_cur: bfloat16 [4, 8192, 2048], P('fsdp', 'ctx'), may hold values from -6 to 6
- cot_next: bfloat16 [4, 8192, 2048], P('fsdp', 'ctx'), may hold values from -6 to 6
- w_q: bfloat16 [2048, 1024], P('fsdp')
- w_kv: bfloat16 [2048, 512], P('fsdp')
- w_out: bfloat16 [2048, 1024], P('fsdp'), may hold values from -0.1875 to 0.1875
Outputs:
- x_prev: bfloat16 [4, 8192, 2048], P('fsdp', 'ctx')
- grad_cur: bfloat16 [4, 8192, 2048], P('fsdp', 'ctx')
- grad_weights: float32 [2048, 2560], P(('ctx', 'fsdp'))
The draws below stay inside these ranges and needn't reach their ends.
All inputs are finite; a program needn't handle non-finite values.
Results may differ from the reference program's by a relative error of at most 0.015.
The reference program's roundings to bfloat16 on the way (of `hidden`, `grad_attn`, `probs_low`, `attended`, `grad_scores`, `grad_query` and `grad_kv`) count: a program that leaves them out, or rounds other values in their place, can miss the bound.
Values may be sent and summed in bfloat16 or wider, within the bound.
No kernel may reach another device: no remote copies, remote signals or barrier semaphores. Data moves between devices by JAX's collectives and lax.ppermute only.
A program may use at most 192 MiB of HBM per device.

```python
import math
import jax
import jax.numpy as jnp
from jax import lax

MODEL_WIDTH = 2048
QUERY_HEADS = 8
KEY_VALUE_HEADS = 2
HEAD_SIZE = 128
WINDOW_TOKENS = 1024
SHARD = 256
SEQS = 4
SEQUENCE_TOKENS = 8192


def query_start_index(key):
    unscaled_scores = jax.random.normal(jax.random.fold_in(key, 101), (MODEL_WIDTH, QUERY_HEADS * HEAD_SIZE), jnp.float32)
    return jnp.clip(unscaled_scores, -6.0, 6.0) * (1.0 / math.sqrt(MODEL_WIDTH))


def draw_w_q(key, part):
    return query_start_index(key).astype(jnp.bfloat16)


def draw_w_kv(key, part):
    unscaled_scores = jax.random.normal(jax.random.fold_in(key, 102), (MODEL_WIDTH, 2 * KEY_VALUE_HEADS * HEAD_SIZE), jnp.float32)
    unscaled_scores = jnp.clip(unscaled_scores, -6.0, 6.0) * (1.0 / math.sqrt(MODEL_WIDTH))
    return unscaled_scores.astype(jnp.bfloat16)


def levels(stream_key, dims, cuts, low, top_value):
    factor_of = 1.0
    for dim, shards_of in cuts:
        steps = jax.random.uniform(jax.random.fold_in(jax.random.fold_in(stream_key, 6), dim), (shards_of,), jnp.float32, low / len(cuts), top_value / len(cuts))
        factor_of = factor_of * jnp.repeat(jnp.exp(steps), dims[dim] // shards_of).reshape((-1,) + (1,) * (len(dims) - 1 - dim))
    return factor_of


def centred(own_key, dims, width, reach, split=(), kind=jnp.bfloat16):
    result = width * jax.random.normal(own_key, dims, jnp.float32)
    if split:
        result = result * levels(own_key, dims, split, -0.22, 0.18)
    return jnp.clip(result, -reach, reach).astype(kind)


def setup_inputs(seed: int = 0) -> dict:
    seeds = jax.random.split(jax.random.key(seed), 8)
    return {
        "x_cur": centred(seeds[0], (SEQS, SEQUENCE_TOKENS, MODEL_WIDTH), 1.0, 6.0, ((0, 4), (1, 32))),
        "x_next": centred(seeds[1], (SEQS, SEQUENCE_TOKENS, MODEL_WIDTH), 1.0, 6.0, ((0, 4), (1, 32))),
        "cot_cur": centred(seeds[2], (SEQS, SEQUENCE_TOKENS, MODEL_WIDTH), 1.0, 6.0, ((0, 4), (1, 32))),
        "cot_next": centred(seeds[3], (SEQS, SEQUENCE_TOKENS, MODEL_WIDTH), 1.0, 6.0, ((0, 4), (1, 32))),
        "w_q": draw_w_q(jax.random.fold_in(seeds[7], 71), 0),
        "w_kv": draw_w_kv(jax.random.fold_in(seeds[7], 71), 0),
        "w_out": centred(seeds[6], (MODEL_WIDTH, QUERY_HEADS * HEAD_SIZE), (QUERY_HEADS * HEAD_SIZE) ** -0.5, 0.1875, ((0, 4),)),
    }


EPS = 1e-05

def normalize(rows):
    values = rows.astype(jnp.float32)
    inv_rms = lax.rsqrt(lax.optimization_barrier(jnp.mean(values * values, axis=-1, keepdims=True)) + EPS)
    return (values * inv_rms, inv_rms)

def window_block(query_rows, key_value_pairs, output_gradient, base):
    window_extent = key_value_pairs.shape[0]
    element_count = query_rows.shape[0]
    query_group = QUERY_HEADS // KEY_VALUE_HEADS
    scale = 1.0 / math.sqrt(HEAD_SIZE)
    query_pos = base + jnp.arange(element_count, dtype=jnp.int32)
    key_pos = base - WINDOW_TOKENS + jnp.arange(window_extent, dtype=jnp.int32)
    offset = query_pos[:, None] - key_pos[None, :]
    allowed = (offset >= 0) & (offset < WINDOW_TOKENS) & (key_pos[None, :] >= 0)
    query_grouped = query_rows.reshape(element_count, KEY_VALUE_HEADS, query_group, HEAD_SIZE).astype(jnp.float32)
    key_tensor = key_value_pairs[:, :KEY_VALUE_HEADS * HEAD_SIZE].reshape(window_extent, KEY_VALUE_HEADS, HEAD_SIZE).astype(jnp.float32)
    value_tensor = key_value_pairs[:, KEY_VALUE_HEADS * HEAD_SIZE:].reshape(window_extent, KEY_VALUE_HEADS, HEAD_SIZE).astype(jnp.float32)
    scores = jnp.einsum('igmd,jgd->gmij', query_grouped, key_tensor) * scale
    scores = jnp.where(allowed[None, None], scores, -jnp.inf)
    top = lax.optimization_barrier(jnp.max(scores, axis=-1, keepdims=True))
    expo = jnp.exp(scores - top)
    probs = expo / lax.optimization_barrier(jnp.sum(expo, axis=-1, keepdims=True))
    probs_low = lax.optimization_barrier(probs.astype(jnp.bfloat16)).astype(jnp.float32)
    attended = jnp.einsum('gmij,jgd->igmd', probs_low, value_tensor)
    gradient_grouped = output_gradient.reshape(element_count, KEY_VALUE_HEADS, query_group, HEAD_SIZE).astype(jnp.float32)
    grad_probs = jnp.einsum('igmd,jgd->gmij', gradient_grouped, value_tensor)
    delta = jnp.einsum('igmd,igmd->gmi', gradient_grouped, attended)
    grad_scores = (probs * (grad_probs - delta[..., None]) * scale).astype(jnp.bfloat16)
    grad_scores = lax.optimization_barrier(grad_scores).astype(jnp.float32)
    grad_query = jnp.einsum('gmij,jgd->igmd', grad_scores, key_tensor).astype(jnp.bfloat16)
    key_gradient = jnp.einsum('gmij,igmd->jgd', grad_scores, query_grouped)
    value_gradient = jnp.einsum('gmij,igmd->jgd', probs_low, gradient_grouped)
    value_partial_sum = jnp.concatenate([key_gradient.reshape(window_extent, KEY_VALUE_HEADS * HEAD_SIZE), value_gradient.reshape(window_extent, KEY_VALUE_HEADS * HEAD_SIZE)], 1)
    return (attended.astype(jnp.bfloat16).reshape(element_count, QUERY_HEADS * HEAD_SIZE), grad_query.reshape(element_count, QUERY_HEADS * HEAD_SIZE), value_partial_sum.astype(jnp.bfloat16))

def reference(x_cur, x_next, cot_cur, cot_next, w_q, w_kv, w_out):
    contract_cols = (((1,), (1,)), ((), ()))
    contract_rows = (((0,), (0,)), ((), ()))
    window_extent = WINDOW_TOKENS + SHARD

    def one_sequence(total, items):
        x_row, next_row, cot_row, cotn_row = items
        normed, inv_rms = normalize(x_row)
        hidden = normed.astype(jnp.bfloat16)
        query_rows = jnp.dot(hidden, w_q, preferred_element_type=jnp.float32).astype(jnp.bfloat16)
        key_value_pairs = jnp.dot(hidden, w_kv, preferred_element_type=jnp.float32).astype(jnp.bfloat16)
        grad_attn = (2.0 * jnp.dot(cotn_row, w_out, preferred_element_type=jnp.float32)).astype(jnp.bfloat16)
        padded_input = jnp.concatenate([jnp.zeros((WINDOW_TOKENS, 2 * KEY_VALUE_HEADS * HEAD_SIZE), key_value_pairs.dtype), key_value_pairs], 0)

        def one_block(accum, index):
            start = (index * SHARD).astype(jnp.int32)
            q_block = lax.dynamic_slice_in_dim(query_rows, start, SHARD, 0)
            kv_block = lax.dynamic_slice_in_dim(padded_input, start, window_extent, 0)
            g_block = lax.dynamic_slice_in_dim(grad_attn, start, SHARD, 0)
            out_block, dq_block, value_partial_sum = window_block(q_block, kv_block, g_block, start)
            current = lax.dynamic_slice_in_dim(accum, start, window_extent, 0)
            accum = lax.dynamic_update_slice_in_dim(accum, current + value_partial_sum.astype(jnp.float32), start, 0)
            return (accum, (out_block, dq_block))
        initial_accumulator = jnp.zeros((WINDOW_TOKENS + SEQUENCE_TOKENS, 2 * KEY_VALUE_HEADS * HEAD_SIZE), jnp.float32)
        accum, (out_blocks, dq_blocks) = lax.scan(one_block, initial_accumulator, jnp.arange(SEQUENCE_TOKENS // SHARD, dtype=jnp.int32))
        attended = out_blocks.reshape(SEQUENCE_TOKENS, QUERY_HEADS * HEAD_SIZE)
        grad_query = dq_blocks.reshape(SEQUENCE_TOKENS, QUERY_HEADS * HEAD_SIZE)
        grad_kv = accum[WINDOW_TOKENS:].astype(jnp.bfloat16)
        layer_out = lax.dot_general(attended, w_out, contract_cols, preferred_element_type=jnp.float32)
        prev_row = (next_row.astype(jnp.float32) - 2.0 * layer_out).astype(jnp.bfloat16)
        grad_hidden = lax.dot_general(grad_query, w_q, contract_cols, preferred_element_type=jnp.float32)
        grad_hidden = grad_hidden + lax.dot_general(grad_kv, w_kv, contract_cols, preferred_element_type=jnp.float32)
        grad_x = inv_rms * (grad_hidden - normed * lax.optimization_barrier(jnp.mean(grad_hidden * normed, axis=-1, keepdims=True)))
        grad_row = (cot_row.astype(jnp.float32) + grad_x).astype(jnp.bfloat16)
        left = jnp.concatenate([grad_query, grad_kv], 1)
        term_in = lax.dot_general(hidden, left, contract_rows, preferred_element_type=jnp.float32)
        term_out = 2.0 * lax.dot_general(cotn_row, attended, contract_rows, preferred_element_type=jnp.float32)
        total = total + jnp.concatenate([term_in, term_out], 1)
        return (total, (prev_row, grad_row))
    initial_total = jnp.zeros((MODEL_WIDTH, 2 * QUERY_HEADS * HEAD_SIZE + 2 * KEY_VALUE_HEADS * HEAD_SIZE), jnp.float32)
    total, (x_prev, grad_cur) = lax.scan(one_sequence, initial_total, (x_cur, x_next, cot_cur, cot_next))
    grad_weights = total * (1.0 / math.sqrt(SEQS * SEQUENCE_TOKENS))
    return (x_prev, grad_cur, grad_weights)
```

```python
import math

import jax
import jax.numpy as jnp
from jax import lax
from jax.sharding import Mesh
from jax.sharding import PartitionSpec as P

QUERY_HEADS = 8
KEY_VALUE_HEADS = 2
HEAD_SIZE = 128
WINDOW_TOKENS = 1024


EPS = 1e-05

CTX = ("x", "z", "yl")
FSDP = ("yh", "c")
CHIPS = ("x", "z", "yl", "yh")


def from_behind(value, axis, steps):
    count = lax.axis_size(axis)
    leading, last = (max(0, -steps), min(count, count - steps))
    return lax.ppermute(value, axis, [(source, source + steps) for source in range(leading, last)])


def swap_cores(value):
    return lax.ppermute(value, "c", [(0, 1), (1, 0)])


def normalize(rows):
    values = rows.astype(jnp.float32)
    inv_rms = lax.rsqrt(jnp.mean(values * values, axis=-1, keepdims=True) + EPS)
    return (values * inv_rms, inv_rms)


def head_block(items, allowed):
    quer3, keys2, vals2, grad3 = items
    scale = 1.0 / math.sqrt(HEAD_SIZE)
    scores = jnp.einsum("imd,jd->mij", quer3, keys2, preferred_element_type=jnp.float32) * scale
    scores = jnp.where(allowed[None], scores, -jnp.inf)
    top = jnp.max(scores, axis=-1, keepdims=True)
    expo = jnp.exp(scores - top)
    probs = expo / jnp.sum(expo, axis=-1, keepdims=True)
    probs_low = probs.astype(jnp.bfloat16)
    attended = jnp.einsum("mij,jd->imd", probs_low, vals2, preferred_element_type=jnp.float32)
    grad_probs = jnp.einsum("imd,jd->mij", grad3, vals2, preferred_element_type=jnp.float32)
    delta = jnp.einsum("imd,imd->mi", grad3.astype(jnp.float32), attended)
    grad_scores = (probs * (grad_probs - delta[..., None]) * scale).astype(jnp.bfloat16)
    grad_query = jnp.einsum("mij,jd->imd", grad_scores, keys2, preferred_element_type=jnp.float32)
    key_gradient = jnp.einsum("mij,imd->jd", grad_scores, quer3, preferred_element_type=jnp.float32)
    value_gradient = jnp.einsum("mij,imd->jd", probs_low, grad3, preferred_element_type=jnp.float32)
    return (
        attended.astype(jnp.bfloat16),
        grad_query.astype(jnp.bfloat16),
        key_gradient.astype(jnp.bfloat16),
        value_gradient.astype(jnp.bfloat16),
    )


def window_block(query_rows, key_value_pairs, output_gradient, base):
    window_extent = key_value_pairs.shape[0]
    element_count = query_rows.shape[0]
    query_group = QUERY_HEADS // KEY_VALUE_HEADS
    query_pos = base + jnp.arange(element_count, dtype=jnp.int32)
    key_pos = base - WINDOW_TOKENS + jnp.arange(window_extent, dtype=jnp.int32)
    offset = query_pos[:, None] - key_pos[None, :]
    allowed = (offset >= 0) & (offset < WINDOW_TOKENS) & (key_pos[None, :] >= 0)
    query_grouped = query_rows.reshape(
        element_count, KEY_VALUE_HEADS, query_group, HEAD_SIZE
    ).transpose(1, 0, 2, 3)
    gradient_grouped = output_gradient.reshape(
        element_count, KEY_VALUE_HEADS, query_group, HEAD_SIZE
    ).transpose(1, 0, 2, 3)
    key_tensor = (
        key_value_pairs[:, : KEY_VALUE_HEADS * HEAD_SIZE]
        .reshape(window_extent, KEY_VALUE_HEADS, HEAD_SIZE)
        .transpose(1, 0, 2)
    )
    value_tensor = (
        key_value_pairs[:, KEY_VALUE_HEADS * HEAD_SIZE :]
        .reshape(window_extent, KEY_VALUE_HEADS, HEAD_SIZE)
        .transpose(1, 0, 2)
    )

    def per_head(items):
        return head_block(items, allowed)

    attended, grad_query, key_gradient, value_gradient = lax.map(
        per_head, (query_grouped, key_tensor, value_tensor, gradient_grouped)
    )
    attended = attended.transpose(1, 0, 2, 3).reshape(element_count, QUERY_HEADS * HEAD_SIZE)
    grad_query = grad_query.transpose(1, 0, 2, 3).reshape(element_count, QUERY_HEADS * HEAD_SIZE)
    key_gradient = key_gradient.transpose(1, 0, 2).reshape(
        window_extent, KEY_VALUE_HEADS * HEAD_SIZE
    )
    value_gradient = value_gradient.transpose(1, 0, 2).reshape(
        window_extent, KEY_VALUE_HEADS * HEAD_SIZE
    )
    value_partial_sum = jnp.concatenate([key_gradient, value_gradient], 1)
    return (attended, grad_query, value_partial_sum)


def shards(x_cur, x_next, cot_cur, cot_next, w_q, w_kv, w_out):
    full_q, full_kv, full_out = (
        lax.all_gather(w_q, FSDP, axis=0, tiled=True),
        lax.all_gather(w_kv, FSDP, axis=0, tiled=True),
        lax.all_gather(w_out, FSDP, axis=0, tiled=True),
    )
    seq_count, shard, width = x_cur.shape
    base = lax.axis_index(CTX) * shard
    preds = WINDOW_TOKENS // shard
    normed, inv_rms = normalize(x_cur)
    hidden = normed.astype(jnp.bfloat16)
    query_rows = jnp.einsum(
        "sid,dc->sic", hidden, full_q, preferred_element_type=jnp.float32
    ).astype(jnp.bfloat16)
    key_value_pairs = jnp.einsum(
        "sid,dc->sic", hidden, full_kv, preferred_element_type=jnp.float32
    ).astype(jnp.bfloat16)
    grad_attn = (
        2.0 * jnp.einsum("sid,dc->sic", cot_next, full_out, preferred_element_type=jnp.float32)
    ).astype(jnp.bfloat16)
    earlier = []
    for hop in range(1, preds + 1):
        earlier.append(from_behind(key_value_pairs, CTX, hop))
    window_keys = jnp.concatenate(earlier[::-1] + [key_value_pairs], axis=1)

    def per_sequence(items):
        q_rows, kv_rows, g_rows = items
        return window_block(q_rows, kv_rows, g_rows, base)

    attended, grad_query, value_partial_sum = lax.map(
        per_sequence, (query_rows, window_keys, grad_attn)
    )
    owned = value_partial_sum[:, WINDOW_TOKENS:].astype(jnp.float32)
    for hop in range(1, preds + 1):
        piece = value_partial_sum[
            :, WINDOW_TOKENS - hop * shard : WINDOW_TOKENS - (hop - 1) * shard
        ]
        owned = owned + from_behind(piece, CTX, -hop).astype(jnp.float32)
    grad_kv = owned.astype(jnp.bfloat16)
    layer_out = jnp.einsum("sic,dc->sid", attended, full_out, preferred_element_type=jnp.float32)
    x_prev = (x_next.astype(jnp.float32) - 2.0 * layer_out).astype(jnp.bfloat16)
    grad_hidden = jnp.einsum("sic,dc->sid", grad_query, full_q, preferred_element_type=jnp.float32)
    grad_hidden = grad_hidden + jnp.einsum(
        "sic,dc->sid", grad_kv, full_kv, preferred_element_type=jnp.float32
    )
    grad_x = inv_rms * (
        grad_hidden - normed * jnp.mean(grad_hidden * normed, axis=-1, keepdims=True)
    )
    grad_cur = (cot_cur.astype(jnp.float32) + grad_x).astype(jnp.bfloat16)
    core = lax.axis_index("c")
    token_total = seq_count * shard * lax.axis_size(CTX) * lax.axis_size(FSDP)
    rows_in = hidden.reshape(seq_count * shard, width)
    rows_out = cot_next.reshape(seq_count * shard, width)
    both_in = jnp.concatenate([rows_in, swap_cores(rows_in)], axis=0)
    both_out = jnp.concatenate([rows_out, swap_cores(rows_out)], axis=0)

    def halves(rows):
        rows = rows.reshape(seq_count * shard, -1)
        half = rows.shape[1] // 2
        first = core == 0
        return (
            jnp.where(first, rows[:, :half], rows[:, half:]),
            jnp.where(first, rows[:, half:], rows[:, :half]),
        )

    kept, sent = zip(halves(grad_query), halves(grad_kv), halves(attended))
    kept = jnp.concatenate(kept, axis=1)
    arrived = swap_cores(jnp.concatenate(sent, axis=1))
    split = grad_query.shape[-1] // 2 + grad_kv.shape[-1] // 2
    left = jnp.concatenate([kept, arrived], axis=0)
    contract_rows = (((0,), (0,)), ((), ()))
    term_in = lax.dot_general(
        both_in, left[:, :split], contract_rows, preferred_element_type=jnp.float32
    )
    term_out = 2.0 * lax.dot_general(
        both_out, left[:, split:], contract_rows, preferred_element_type=jnp.float32
    )
    terms = jnp.concatenate([term_in, term_out], axis=1).astype(jnp.bfloat16)
    chips = lax.axis_size(CHIPS)
    terms = terms.reshape(chips, width // chips, -1)
    terms = lax.all_to_all(terms, CHIPS, 0, 0)
    summed = jnp.sum(terms.astype(jnp.float32), axis=0) * (1.0 / math.sqrt(token_total))
    mine = summed.shape[0] // 2
    upper = jnp.where(core == 0, summed[:mine], summed[mine:])
    lower = swap_cores(jnp.where(core == 0, summed[mine:], summed[:mine]))
    zero = jnp.where(core == 0, upper, lower)
    one = jnp.where(core == 0, lower, upper)
    q_half = grad_query.shape[-1] // 2
    grad_weights = jnp.concatenate(
        [
            zero[:, :q_half],
            one[:, :q_half],
            zero[:, q_half:split],
            one[:, q_half:split],
            zero[:, split:],
            one[:, split:],
        ],
        axis=1,
    )
    return (x_prev, grad_cur, grad_weights)


def solution(mesh):
    mesh = Mesh(mesh.devices.reshape(4, 4, 2, 2, 2), CTX + FSDP)
    in_specs = (
        P(FSDP, CTX, None),
        P(FSDP, CTX, None),
        P(FSDP, CTX, None),
        P(FSDP, CTX, None),
        P(FSDP, None),
        P(FSDP, None),
        P(FSDP, None),
    )
    out_specs = (P(FSDP, CTX, None), P(FSDP, CTX, None), P(CTX + FSDP, None))
    return jax.shard_map(shards, mesh=mesh, in_specs=in_specs, out_specs=out_specs, check_vma=False)
```

```python
import math

import jax
import jax.numpy as jnp
from jax import lax
from jax.experimental import pallas as pl
from jax.experimental.pallas import tpu as pltpu
from jax.sharding import Mesh
from jax.sharding import PartitionSpec as P

QUERY_HEADS = 8
KEY_VALUE_HEADS = 2
HEAD_SIZE = 128
WINDOW_TOKENS = 1024
GROUP = QUERY_HEADS // KEY_VALUE_HEADS
SCALE = 1.0 / math.sqrt(HEAD_SIZE)
LANES = 128
EPS = 1e-05

CTX = ("x", "z", "yl")
FSDP = ("yh", "c")
CHIPS = ("x", "z", "yl", "yh")
QUARTERS = (0, 3, 1, 2)

F32 = jnp.float32
BF16 = jnp.bfloat16
VMEM = pl.BlockSpec(memory_space=pltpu.VMEM)
SMEM = pl.BlockSpec(memory_space=pltpu.SMEM)


def call(kernel, outs, n_scalar, args, flops, scratch=(), limit=24):
    moved = sum(a.size * a.dtype.itemsize for a in args) + sum(
        math.prod(o.shape) * o.dtype.itemsize for o in outs
    )
    return pl.pallas_call(
        kernel,
        out_shape=outs,
        in_specs=[SMEM] * n_scalar + [VMEM] * (len(args) - n_scalar),
        out_specs=[VMEM] * len(outs),
        scratch_shapes=list(scratch),
        cost_estimate=pl.CostEstimate(flops=flops, bytes_accessed=moved, transcendentals=0),
        compiler_params=pltpu.CompilerParams(vmem_limit_bytes=limit * 2**20),
    )(*args)


def array(shape, dtype):
    return jax.ShapeDtypeStruct(shape, dtype)


def dot(a, b, dims):
    return lax.dot_general(a, b, (dims, ((), ())), preferred_element_type=F32)


NN = ((1,), (0,))
NT = ((1,), (1,))


def swap_cores(value):
    return lax.ppermute(value, "c", [(0, 1), (1, 0)])


def swap_low(value):
    return lax.ppermute(value, "yl", [(0, 1), (1, 0)])


def along(value, axis, step):
    count = lax.axis_size(axis)
    return lax.ppermute(value, axis, [(i, (i + step) % count) for i in range(count)])


def shift(value, step):
    count = lax.axis_size(("x", "z"))
    pairs = [(i, i + step) for i in range(count) if 0 <= i + step < count]
    return lax.ppermute(value, ("x", "z"), pairs)


def fetch(value):
    return lax.ppermute(value, ("yl", "yh"), [(0, 3), (3, 0), (1, 2), (2, 1)])


def gather_kv(shard):
    far = fetch(shard)
    other = swap_cores(shard)
    return (shard, other, far, swap_cores(far))


def gather_qo(w_q, w_out, colour):
    rows = w_q.shape[0] // 4
    piece = jnp.concatenate(
        [lax.dynamic_slice_in_dim(w, colour * rows, rows, 0) for w in (w_q, w_out)], axis=1
    )
    piece = fetch(piece)
    left = along(piece, "x", 1)
    right = along(piece, "x", -1)
    ahead = along(piece, "z", -1)
    shard = jnp.concatenate([w_q, w_out], axis=1)
    other = swap_cores(shard)
    far = jnp.concatenate([piece, left, right, ahead], axis=0)
    return (shard, other, far, swap_cores(far))


def normalize(x):
    values = x.astype(F32)
    inv_rms = lax.rsqrt(jnp.mean(values * values, axis=-1, keepdims=True) + EPS)
    return values * inv_rms, inv_rms


def block(place, j):
    return pl.ds(pl.multiple_of(place[j] * LANES, LANES), LANES)


def whole(place, i, depth):
    return pl.ds(pl.multiple_of(place[16 + i] * depth, depth), depth)


def prepare_kernel(place, x_ref, c_ref, hidden_ref, hp_ref, cp_ref, ht_ref, ct_ref):
    normed, _ = normalize(x_ref[...])
    hidden_ref[...] = normed.astype(BF16)
    for j in range(hp_ref.shape[1] // LANES):
        to = slice(j * LANES, (j + 1) * LANES)
        hp_ref[:, to] = hidden_ref[:, block(place, j)]
        cp_ref[:, to] = c_ref[:, block(place, j)]
        ht_ref[to, :] = hidden_ref[:, to].T
        ct_ref[to, :] = c_ref[:, to].T


def project(rows_ref, shards, columns):
    depth = shards[0].shape[0]
    total = None
    for i, shard in enumerate(shards):
        term = dot(rows_ref[:, i * depth : (i + 1) * depth], shard[:, columns], NN)
        total = term if total is None else total + term
    return total


def kv_kernel(place, hidden_ref, s0, s1, s2, s3, out_ref):
    depth = s0.shape[0]
    total = None
    for i, shard in enumerate((s0, s1, s2, s3)):
        term = dot(hidden_ref[:, whole(place, i, depth)], shard[...], NN)
        total = term if total is None else total + term
    out_ref[...] = total.astype(BF16)


def query_kernel(hp_ref, cp_ref, s0, s1, s2, s3, q_ref, g_ref):
    width = q_ref.shape[1]
    shards = (s0, s1, s2, s3)
    q_ref[...] = project(hp_ref, shards, slice(0, width)).astype(BF16)
    g_ref[...] = (2.0 * project(cp_ref, shards, slice(width, 2 * width))).astype(BF16)


def attention_kernel(
    where, q_ref, g_ref, k4, k3, k2, k1, k0,
    att_ref, dq_ref, t4, t3, t2, t1, t0,
    kt_ref, vt_ref, e_ref, dk_ref, dv_ref,
):
    shard = q_ref.shape[0]
    ctx, group = where[0], where[1]
    pieces, terms = (k4, k3, k2, k1, k0), (t4, t3, t2, t1, t0)
    count = len(pieces)
    log2e = SCALE * math.log2(math.e)
    key = lax.broadcasted_iota(jnp.int32, (shard, shard), 0)
    query = lax.broadcasted_iota(jnp.int32, (shard, shard), 1)
    kcol = pl.ds(pl.multiple_of(group * HEAD_SIZE, HEAD_SIZE), HEAD_SIZE)
    vcol = pl.ds(pl.multiple_of((KEY_VALUE_HEADS + group) * HEAD_SIZE, HEAD_SIZE), HEAD_SIZE)
    for b, piece in enumerate(pieces):
        rows = slice(b * shard, (b + 1) * shard)
        kt_ref[:, rows] = piece[:, kcol].T
        vt_ref[:, rows] = piece[:, vcol].T
    dk_ref[...] = jnp.zeros_like(dk_ref)
    dv_ref[...] = jnp.zeros_like(dv_ref)

    @pl.loop(0, GROUP)
    def _(m):
        column = pl.ds(pl.multiple_of((group * GROUP + m) * HEAD_SIZE, HEAD_SIZE), HEAD_SIZE)
        q, grad = q_ref[:, column], g_ref[:, column]
        top = None
        for b, piece in enumerate(pieces):
            s = dot(piece[:, kcol], q, NT)
            if b == 0:
                s = jnp.where(key > query, s, -jnp.inf)
            if b == count - 1:
                s = jnp.where(key <= query, s, -jnp.inf)
            e_ref[b * shard : (b + 1) * shard, :] = s
            best = jnp.max(s, axis=0, keepdims=True)
            if b < count - 1:
                best = jnp.where(ctx >= count - 1 - b, best, -jnp.inf)
            top = best if top is None else jnp.maximum(top, best)
        total = None
        for b in range(count):
            rows = slice(b * shard, (b + 1) * shard)
            base = top * log2e
            if b < count - 1:
                base = jnp.where(ctx >= count - 1 - b, base, jnp.inf)
            e = jnp.exp2(e_ref[rows, :] * log2e - base)
            e_ref[rows, :] = e
            part = jnp.sum(e, axis=0, keepdims=True)
            total = part if total is None else total + part
        inverse = 1.0 / total
        out = None
        for b in range(count):
            rows = slice(b * shard, (b + 1) * shard)
            low = (e_ref[rows, :] * inverse).astype(BF16)
            term = dot(vt_ref[:, rows], low, NN)
            out = term if out is None else out + term
            dv_ref[rows, :] += dot(low, grad, NN)
        delta = jnp.sum(grad.astype(F32).T * out, axis=0, keepdims=True)
        factor = inverse * SCALE
        grad_q = None
        for b, piece in enumerate(pieces):
            rows = slice(b * shard, (b + 1) * shard)
            gp = dot(piece[:, vcol], grad, NT)
            gs = ((gp - delta) * factor * e_ref[rows, :]).astype(BF16)
            term = dot(kt_ref[:, rows], gs, NN)
            grad_q = term if grad_q is None else grad_q + term
            dk_ref[rows, :] += dot(gs, q, NN)
        here = pl.ds(pl.multiple_of(m * HEAD_SIZE, HEAD_SIZE), HEAD_SIZE)
        att_ref[:, here] = out.T.astype(BF16)
        dq_ref[:, here] = grad_q.T.astype(BF16)

    for b, term in enumerate(terms):
        rows = slice(b * shard, (b + 1) * shard)
        term[:, :HEAD_SIZE] = dk_ref[rows, :].astype(BF16)
        term[:, HEAD_SIZE:] = dv_ref[rows, :].astype(BF16)


def weights_kernel(ht, hto, ct, cto, dq, dqo, att, atto, out_ref):
    width = dq.shape[1]
    out_ref[:, :width] = (dot(ht[...], dq[...], NN) + dot(hto[...], dqo[...], NN)).astype(BF16)
    term = dot(ct[...], att[...], NN) + dot(cto[...], atto[...], NN)
    out_ref[:, width : 2 * width] = (2.0 * term).astype(BF16)


def fill_kernel(ht, hto, dkv, dkvo, _, out_ref, term_ref, sem):
    begin = out_ref.shape[1] - dkv.shape[1]
    term_ref[...] = (dot(ht[...], dkv[...], NN) + dot(hto[...], dkvo[...], NN)).astype(BF16)
    copy = pltpu.make_async_copy(term_ref, out_ref.at[:, begin:], sem)
    copy.start()
    copy.wait()


def previous_kernel(place, where, att, atto, next_ref, s0, s1, s2, s3, out_ref):
    half = att.shape[1]
    depth = s0.shape[0]
    for i, shard in enumerate((s0, s1, s2, s3)):
        term = dot(att[...], shard[:, group_columns(where[1], 2 * half, half)], NT)
        term += dot(atto[...], shard[:, group_columns(1 - where[1], 2 * half, half)], NT)
        for p in range(depth // LANES):
            to = block(place, i * (depth // LANES) + p)
            part = term[:, p * LANES : (p + 1) * LANES]
            out_ref[:, to] = (next_ref[:, to].astype(F32) - 2.0 * part).astype(BF16)


def group_columns(group, begin, width):
    return pl.ds(pl.multiple_of(begin + group * width, width), width)


def current_kernel(
    place, where, dq, dqo, dkv, dkvo, x_ref, cot_ref, q0, q1, q2, q3, k0, k1, k2, k3, out_ref, gh_ref
):
    half = dq.shape[1]
    depth = q0.shape[0]
    for i, shard in enumerate((q0, q1, q2, q3)):
        term = dot(dq[...], shard[:, group_columns(where[1], 0, half)], NT)
        term += dot(dqo[...], shard[:, group_columns(1 - where[1], 0, half)], NT)
        for p in range(depth // LANES):
            to = block(place, i * (depth // LANES) + p)
            gh_ref[:, to] = term[:, p * LANES : (p + 1) * LANES]
    for i, shard in enumerate((k0, k1, k2, k3)):
        to = whole(place, i, depth)
        term = gh_ref[:, to]
        for group, part in ((where[1], dkv), (1 - where[1], dkvo)):
            for begin in (0, HEAD_SIZE):
                columns = group_columns(group, KEY_VALUE_HEADS * begin, HEAD_SIZE)
                term += dot(part[:, begin : begin + HEAD_SIZE], shard[:, columns], NT)
        gh_ref[:, to] = term
    normed, inv_rms = normalize(x_ref[...])
    grad_hidden = gh_ref[...]
    mean = jnp.mean(grad_hidden * normed, axis=-1, keepdims=True)
    grad_x = inv_rms * (grad_hidden - normed * mean)
    out_ref[...] = (cot_ref[...].astype(F32) + grad_x).astype(BF16)


def sum_kernel(norm, where, terms, kept_ref, sent_ref, total):
    total[...] = terms[0].astype(F32)

    @pl.loop(1, terms.shape[0])
    def _(i):
        total[...] += terms[i].astype(F32)

    own = kept_ref.shape[0]
    kept_ref[...] = total[pl.ds(pl.multiple_of(where[1] * own, own), own), :] * norm
    sent_ref[...] = total[pl.ds(pl.multiple_of((1 - where[1]) * own, own), own), :] * norm


def assemble_kernel(where, kept, came, out_ref):
    half = GROUP * HEAD_SIZE
    ends = 2 * half + 2 * KEY_VALUE_HEADS * HEAD_SIZE
    for side, rows in ((where[1], kept), (1 - where[1], came)):
        out_ref[:, group_columns(side, 0, half)] = rows[:, :half]
        out_ref[:, group_columns(side, ends, half)] = rows[:, half : 2 * half]
        for i in range(2):
            to = group_columns(side, 2 * half + i * KEY_VALUE_HEADS * HEAD_SIZE, HEAD_SIZE)
            begin = 2 * half + i * HEAD_SIZE
            out_ref[:, to] = rows[:, begin : begin + HEAD_SIZE]


def shards(x_cur, x_next, cot_cur, cot_next, w_q, w_kv, w_out):
    seq_count, shard, width = x_cur.shape
    x_cur, x_next, cot_cur, cot_next = (
        v.reshape(seq_count * shard, width) for v in (x_cur, x_next, cot_cur, cot_next)
    )
    q_width, kv_width, depth = w_q.shape[1], w_kv.shape[1], w_q.shape[0]
    x, z, low, high, core = (lax.axis_index(a) for a in ("x", "z", "yl", "yh", "c"))
    ctx = lax.axis_index(CTX)
    token_total = seq_count * shard * lax.axis_size(CTX) * lax.axis_size(FSDP)
    colour = (x + 2 * z) % 4
    mine = 2 * high + core
    apart = 2 * (1 - high) + core
    per = depth // LANES
    place = jnp.stack(
        [mine * per + i for i in range(per)]
        + [(mine ^ 1) * per + i for i in range(per)]
        + [apart * per + (colour + i) % 4 for i in QUARTERS]
        + [(apart ^ 1) * per + (colour + i) % 4 for i in QUARTERS]
        + [mine, mine ^ 1, apart, apart ^ 1]
    ).astype(jnp.int32)

    kv_shards = gather_kv(w_kv)
    qo_shards = gather_qo(w_q, w_out, colour)

    rows = array((shard, width), BF16)
    turned = array((width, shard), BF16)
    hidden, hidden_placed, cot_placed, hidden_t, cot_t = call(
        prepare_kernel, [rows] * 3 + [turned] * 2, 1, [place, x_cur, cot_next], 8 * shard * width
    )
    (kv,) = call(
        kv_kernel,
        [array((shard, kv_width), BF16)],
        1,
        [place, hidden, *kv_shards],
        2 * shard * width * kv_width,
    )
    behind2 = shift(kv, 1)
    behind4 = shift(behind2, 1)
    behind2, crossing = lax.optimization_barrier((behind2, jnp.where(low == 0, kv, behind2)))
    behind1 = swap_low(crossing)
    crossing = jnp.where(low == 0, behind2, behind4)
    behind3 = swap_low(crossing)

    queries, grad_attn = call(
        query_kernel,
        [array((shard, q_width), BF16)] * 2,
        0,
        [hidden_placed, cot_placed, *qo_shards],
        4 * shard * width * q_width,
    )
    hidden_to = swap_cores(hidden_t)
    cot_to = swap_cores(cot_t)

    keys = shard + WINDOW_TOKENS
    half_q, half_kv = q_width // 2, kv_width // 2
    where = jnp.stack([ctx, core]).astype(jnp.int32)
    windows = [behind4, behind3, behind2, behind1, kv]

    def attend(which):
        att, dq, *terms = call(
            attention_kernel,
            [array((shard, half_q), BF16)] * 2 + [array((shard, half_kv), BF16)] * 5,
            1,
            [jnp.stack([ctx, which]).astype(jnp.int32), queries, grad_attn, *windows],
            6 * shard * keys * q_width,
            [
                pltpu.VMEM((HEAD_SIZE, keys), BF16),
                pltpu.VMEM((HEAD_SIZE, keys), BF16),
                pltpu.VMEM((keys, shard), F32),
                pltpu.VMEM((keys, HEAD_SIZE), F32),
                pltpu.VMEM((keys, HEAD_SIZE), F32),
            ],
        )
        return att, dq, terms

    def cross(terms):
        _, t3, _, t1, _ = terms
        third = swap_low(t3)
        first = swap_low(t1)
        return third, first

    def gather_terms(terms, crossed):
        t4, _, t2, _, t0, third, first = (v.astype(F32) for v in (*terms, *crossed))
        two_back = (t4 + jnp.where(low == 0, 0.0, third)).astype(BF16)
        two_back = shift(two_back, -1)
        one_back = t2 + jnp.where(low == 0, third, first) + two_back.astype(F32)
        one_back = one_back.astype(BF16)
        one_back = shift(one_back, -1)
        grad_kv = t0 + jnp.where(low == 0, first, 0.0) + one_back.astype(F32)
        return grad_kv.astype(BF16)

    att_sent, dq_sent, terms_sent = attend(1 - core)
    dq_came = swap_cores(dq_sent)
    att_came = swap_cores(att_sent)
    crossed = cross(terms_sent)
    att_kept, dq_kept, terms_kept = attend(core)
    dkv_sent = gather_terms(terms_sent, crossed)
    dkv_kept = gather_terms(terms_kept, cross(terms_kept))
    dkv_came = swap_cores(dkv_sent)

    chips = lax.axis_size(CHIPS)
    columns = q_width + half_kv
    (terms,) = call(
        weights_kernel,
        [array((width, columns), BF16)],
        0,
        [hidden_t, hidden_to, cot_t, cot_to, dq_kept, dq_came, att_kept, att_came],
        4 * shard * width * q_width,
    )
    turned_flops = 4 * shard * width * half_kv
    terms = pl.pallas_call(
        fill_kernel,
        name="fill_kernel",
        out_shape=array((width, columns), BF16),
        in_specs=[VMEM] * 4 + [pl.BlockSpec(memory_space=pl.ANY)],
        out_specs=pl.BlockSpec(memory_space=pl.ANY),
        scratch_shapes=[pltpu.VMEM((width, half_kv), BF16), pltpu.SemaphoreType.DMA(())],
        input_output_aliases={4: 0},
        cost_estimate=pl.CostEstimate(
            flops=turned_flops, bytes_accessed=4 * width * shard, transcendentals=0
        ),
        compiler_params=pltpu.CompilerParams(vmem_limit_bytes=16 * 2**20),
    )(hidden_t, hidden_to, dkv_kept, dkv_came, terms)
    terms = lax.all_to_all(terms.reshape(chips, width // chips, columns), CHIPS, 0, 0)

    (x_prev,) = call(
        previous_kernel,
        [rows],
        2,
        [place, where, att_kept, att_sent, x_next, *qo_shards],
        2 * shard * width * q_width,
    )
    (grad_cur,) = call(
        current_kernel,
        [rows],
        2,
        [place, where, dq_kept, dq_sent, dkv_kept, dkv_sent, x_cur, cot_cur]
        + [*qo_shards, *kv_shards],
        2 * shard * width * (q_width + kv_width),
        [pltpu.VMEM((shard, width), F32)],
    )

    own = width // chips // 2
    part = array((own, columns), F32)
    kept, sent = call(
        lambda *refs: sum_kernel(1.0 / math.sqrt(token_total), *refs),
        [part] * 2,
        1,
        [where, terms],
        width * columns,
        [pltpu.VMEM((2 * own, columns), F32)],
    )
    came = swap_cores(sent)
    (grad_weights,) = call(
        assemble_kernel, [array((own, 2 * columns), F32)], 1, [where, kept, came], own * columns
    )
    full = (seq_count, shard, width)
    return (x_prev.reshape(full), grad_cur.reshape(full), grad_weights)


def solution(mesh):
    mesh = Mesh(mesh.devices.reshape(4, 4, 2, 2, 2), CTX + FSDP)
    in_specs = (P(FSDP, CTX, None),) * 4 + (P(FSDP, None),) * 3
    out_specs = (P(FSDP, CTX, None), P(FSDP, CTX, None), P(CTX + FSDP, None))
    return jax.shard_map(shards, mesh=mesh, in_specs=in_specs, out_specs=out_specs, check_vma=False)
```
